32 devices in a mesh: segment: 4 (over y, x), dp: 8 (over z, core).
Axes of the slice: x: 2, y: 2, z: 4, core: 2. Of those that a mesh axis runs over, the one named last changes fastest.
Arguments:
- inputs: bfloat16 [3584, 8192], P('dp'), may hold values from -6 to 6
- cotangent: bfloat16 [3584, 8192], P('dp'), may hold values from -11 to 11
- adapter_down: bfloat16 [4, 128, 8192], P('segment'), may hold values from -0.0625 to 0.0625
- adapter_up: bfloat16 [4, 8192, 128], P('segment'), may hold values from -0.5 to 0.5
- domain_ids: int32 [64], replicated, may hold values from 0 to 8, as said below
- prior_weights: float32 [8], replicated, may hold values from 0.2 to 1
Outputs:
- domain_weights: float32 [8], replicated
- reweighted: float32 [4, 128, 8192], P('segment', None, 'dp')
The draws below stay inside these ranges and needn't reach their ends.
Inputs may be any that keep to these rules, and one draw needn't show every extreme that they name: `domain_ids`: each of the 9 domains names 7 or 8 micro-batches; domain 8 is the generalization domain.
All inputs are finite; a program needn't handle non-finite values.
Results may differ from the reference program's by a relative error of at most 0.02.
Values may be sent and summed in bfloat16 or wider, within the bound.
No kernel may reach another device: no remote copies, remote signals or barrier semaphores. Data moves between devices by JAX's collectives and lax.ppermute only.
A program may use at most 128 MiB of HBM per device.

```python
import math
import jax
import jax.numpy as jnp
from jax import lax

D = 8192
RANK = 128
DOMAINS = 9
MICRO_DEV = 8
TOK_MICRO = 56
TRAIN = 8
SEGMENTS = 4
MICROS = 64
TOKENS = 3584
N_DP = 8


def draw_domain_ids(key, part):
    order = jax.random.permutation(jax.random.fold_in(key, 11), MICROS)
    return (order % DOMAINS).astype(jnp.int32)


def draw_cotangent(key, part):
    noise_key = jax.random.fold_in(key, 23)
    row_place = jnp.arange(TOKENS, dtype=jnp.float32) / TOKENS
    base = jnp.clip(jax.random.normal(noise_key, (TOKENS, D), jnp.float32), -6.0, 6.0)
    return (base * (3.0 ** row_place)[:, None] / 1.7).astype(jnp.bfloat16)


def shard_levels(key, dims, split, low, largest):
    factor_of, own = 1.0, jax.random.fold_in(key, 6)
    for position, parts in split:
        draws = jnp.exp(jax.random.uniform(jax.random.fold_in(own, position), (parts,), jnp.float32, low / len(split), largest / len(split)))
        factor_of = factor_of * jnp.repeat(draws, dims[position] // parts).reshape([-1 if axis == position else 1 for axis in range(len(dims))])
    return factor_of


def noise(key, shape, width, most, shards=(), held_as=jnp.bfloat16):
    result = width * jax.random.normal(key, shape, jnp.float32)
    if shards:
        result = result * shard_levels(key, shape, shards, -0.22, 0.18)
    return jnp.clip(result, -most, most).astype(held_as)


def setup_inputs(seed: int = 0) -> dict:
    splits = jax.random.split(jax.random.key(seed), 7)
    return {
        "inputs": noise(splits[0], (TOKENS, D), 1.0, 6.0, ((0, 8),)),
        "cotangent": draw_cotangent(jax.random.fold_in(splits[6], 71), 0),
        "adapter_down": noise(splits[2], (SEGMENTS, RANK, D), D ** -0.5, 0.0625, ((0, 4),)),
        "adapter_up": noise(splits[3], (SEGMENTS, D, RANK), RANK ** -0.5, 0.5, ((0, 4),)),
        "domain_ids": draw_domain_ids(jax.random.fold_in(splits[6], 71), 0),
        "prior_weights": jnp.clip(jnp.exp(jax.random.uniform(splits[5], (TRAIN,), jnp.float32, math.log(0.2), math.log(1.0))), 0.2, 1.0),
    }


smoothing = 0.5

def silu_slope(preact):
    sigmoid_value = jax.nn.sigmoid(preact)
    return sigmoid_value * (1.0 + preact * (1.0 - sigmoid_value))

def reference(inputs, cotangent, adapter_down, adapter_up, domain_ids, prior_weights):
    segment_inputs = []
    segment_pre = []
    current = inputs
    for section in range(SEGMENTS):
        hidden_pre = jnp.dot(current, adapter_down[section].T, preferred_element_type=jnp.float32)
        hidden_act = jax.nn.silu(hidden_pre).astype(jnp.bfloat16)
        segment_inputs.append(current)
        segment_pre.append(hidden_pre)
        lifted = jnp.dot(hidden_act, adapter_up[section].T, preferred_element_type=jnp.float32)
        current = (current.astype(jnp.float32) + lifted).astype(jnp.bfloat16)
    delta_block = cotangent
    inner_list = [None] * SEGMENTS
    for section in reversed(range(SEGMENTS)):
        pulled_back = jnp.dot(delta_block, adapter_up[section], preferred_element_type=jnp.float32)
        inner_grad = (pulled_back * silu_slope(segment_pre[section])).astype(jnp.bfloat16)
        inner_list[section] = inner_grad
        pushed = jnp.dot(inner_grad, adapter_down[section], preferred_element_type=jnp.float32)
        delta_block = (delta_block.astype(jnp.float32) + pushed).astype(jnp.bfloat16)
    domain_range = jnp.arange(DOMAINS, dtype=jnp.int32)
    onehot = (domain_ids[:, None] == domain_range[None, :]).astype(jnp.float32)
    counts = lax.optimization_barrier(jnp.sum(onehot, axis=0))
    inverse_size = 1.0 / (counts * TOK_MICRO)
    micro_mix = (onehot * inverse_size[None, :]).reshape(N_DP, MICRO_DEV, DOMAINS)
    stacked_inputs = jnp.stack(segment_inputs).reshape(SEGMENTS, N_DP, MICRO_DEV, TOK_MICRO, D)
    stacked_inner = jnp.stack(inner_list).reshape(SEGMENTS, N_DP, MICRO_DEV, TOK_MICRO, RANK)

    def add_owner(total_grad, owner_slot):
        owner_parts = []
        for section in range(SEGMENTS):
            per_micro = jnp.einsum('mtr,mtd->mrd', stacked_inner[section, owner_slot].astype(jnp.float32), stacked_inputs[section, owner_slot].astype(jnp.float32), precision=lax.Precision.HIGHEST)
            owner_part = jnp.einsum('mi,mrd->ird', micro_mix[owner_slot], per_micro, precision=lax.Precision.HIGHEST).astype(jnp.bfloat16)
            owner_part = lax.optimization_barrier(owner_part)
            owner_parts.append(owner_part.astype(jnp.float32))
        return (total_grad + jnp.stack(owner_parts), None)
    zero_grad = jnp.zeros((SEGMENTS, DOMAINS, RANK, D), jnp.float32)
    total_grad, _ = lax.scan(add_owner, zero_grad, jnp.arange(N_DP, dtype=jnp.int32))
    train_grads = total_grad[:, :DOMAINS - 1]
    gen_grad = total_grad[:, DOMAINS - 1]
    scores = lax.optimization_barrier(jnp.sum(train_grads * gen_grad[:, None], axis=(0, 2, 3)))
    mean_gen = jnp.mean(gen_grad * gen_grad)
    total_entries = SEGMENTS * RANK * D
    scaled_scores = scores / (jnp.sqrt(jnp.float32(total_entries)) * (mean_gen + 1e-06))
    raised = prior_weights * jnp.exp(4.0 * jnp.tanh(scaled_scores / 4.0))
    weights_new = smoothing / (DOMAINS - 1) + (1.0 - smoothing) * raised / jnp.sum(raised)
    reweighted = jnp.einsum('i,sird->srd', weights_new, train_grads, precision=lax.Precision.HIGHEST)
    return (weights_new, reweighted)
```

```python
import functools

import jax
import jax.numpy as jnp
import numpy as np
from jax import lax
from jax.experimental import pallas as pl
from jax.experimental.pallas import tpu as pltpu
from jax.sharding import PartitionSpec as P

SMOOTHING = 0.5
BF16 = jnp.bfloat16
F32 = jnp.float32


def swap(array, axis, flip):
    size = lax.axis_size(axis)
    return lax.ppermute(array, axis, [(i, i ^ flip) for i in range(size)])


def bits_of(size):
    return [1 << b for b in range(size.bit_length() - 1)]


def all_sum(array, axis, wire=BF16):
    for flip in bits_of(lax.axis_size(axis)):
        array = array + swap(array.astype(wire), axis, flip).astype(F32)
    return array


def reversed_bits(size):
    width = size.bit_length() - 1
    return np.array([int(format(p, f"0{width}b")[::-1], 2) if width else 0 for p in range(size)], np.int32)


def sigmoid(v):
    return 1.0 / (1.0 + jnp.exp(-v))


def nt(a, b):
    return lax.dot_general(a, b, (((1,), (1,)), ((), ())), preferred_element_type=F32)


def nn(a, b):
    return lax.dot_general(a, b, (((1,), (0,)), ((), ())), preferred_element_type=F32)


def tn(a, b):
    return lax.dot_general(a, b, (((0,), (0,)), ((), ())), preferred_element_type=F32)


def recurrence_kernel(sections, rank, where, *refs):
    pairs = refs[:sections]
    links = refs[sections : 2 * sections]
    inner_out, act_out = refs[2 * sections : 2 * sections + 2]
    pair_at, link_at, pre_at, inner_at = refs[2 * sections + 2 :]
    own = where[0]
    for e in range(sections):
        pair_at[own ^ e] = pairs[e][...]
        link_at[own ^ e] = links[e][...]
    for s in range(sections):
        pre = pair_at[s, :, :rank].astype(F32)
        for r in range(s):
            pre = pre + nn(act_out[r], link_at[s, (r ^ s) - 1])
        pre_at[s] = pre
        act_out[s] = (pre * sigmoid(pre)).astype(BF16)
    for s in reversed(range(sections)):
        pulled = pair_at[s, :, rank:].astype(F32)
        for r in range(s + 1, sections):
            pulled = pulled + nt(inner_at[r], link_at[r, (r ^ s) - 1])
        pre = pre_at[s]
        gate = sigmoid(pre)
        inner_at[s] = (pulled * (gate * (1.0 + pre * (1.0 - gate)))).astype(BF16)
    inner_out[...] = inner_at[own]


def recurrence(own, pairs, links):
    sections = len(pairs)
    rows, rank = pairs[0].shape[0], pairs[0].shape[1] // 2
    vmem = pl.BlockSpec(memory_space=pltpu.VMEM)
    return pl.pallas_call(
        functools.partial(recurrence_kernel, sections, rank),
        out_shape=(
            jax.ShapeDtypeStruct((rows, rank), BF16),
            jax.ShapeDtypeStruct((sections, rows, rank), BF16),
        ),
        in_specs=[pl.BlockSpec(memory_space=pltpu.SMEM)] + [vmem] * (2 * sections),
        out_specs=(vmem, vmem),
        scratch_shapes=[
            pltpu.VMEM((sections, rows, 2 * rank), BF16),
            pltpu.VMEM((sections, sections - 1, rank, rank), BF16),
            pltpu.VMEM((sections, rows, rank), F32),
            pltpu.VMEM((sections, rows, rank), BF16),
        ],
        name="recurrence",
    )(own, *pairs, *links)


def outer_kernel(order, w_ref, x_ref, o_ref):
    o_ref[0] = tn(w_ref[...], x_ref[...]).astype(o_ref.dtype)


def outer_blocks(order, weighted, tokens, width):
    count, rows, rank = order.shape[0], weighted.shape[0], weighted.shape[1]
    return pl.pallas_call(
        outer_kernel,
        out_shape=jax.ShapeDtypeStruct((count, rank, width), BF16),
        grid_spec=pltpu.PrefetchScalarGridSpec(
            num_scalar_prefetch=1,
            grid=(count,),
            in_specs=[
                pl.BlockSpec((rows, rank), lambda k, o: (0, 0)),
                pl.BlockSpec((rows, width), lambda k, o: (0, o[k])),
            ],
            out_specs=pl.BlockSpec((1, rank, width), lambda k, o: (k, 0, 0)),
        ),
        cost_estimate=pl.CostEstimate(
            flops=2 * count * rows * rank * width,
            bytes_accessed=2 * count * width * (rows + rank),
            transcendentals=0,
        ),
        name="outer_blocks",
    )(order, weighted, tokens)


def project_kernel(order, g_ref, x_ref, o_ref):
    @pl.when(pl.program_id(0) == 0)
    def _():
        o_ref[...] = jnp.zeros_like(o_ref)

    o_ref[...] += nt(x_ref[...], g_ref[0])


def project_blocks(order, grads, tokens):
    count, rank, width = grads.shape
    rows = tokens.shape[0]
    return pl.pallas_call(
        project_kernel,
        out_shape=jax.ShapeDtypeStruct((rows, rank), F32),
        grid_spec=pltpu.PrefetchScalarGridSpec(
            num_scalar_prefetch=1,
            grid=(count,),
            in_specs=[
                pl.BlockSpec((1, rank, width), lambda k, o: (k, 0, 0)),
                pl.BlockSpec((rows, width), lambda k, o: (0, o[k])),
            ],
            out_specs=pl.BlockSpec((rows, rank), lambda k, o: (0, 0)),
        ),
        cost_estimate=pl.CostEstimate(
            flops=2 * count * rows * rank * width,
            bytes_accessed=2 * count * width * (rows + rank),
            transcendentals=0,
        ),
        name="project_blocks",
    )(order, grads, tokens)


def scatter_sum(order, weighted, tokens, width):
    size = order.shape[0]
    flips = bits_of(size)
    half = size // 2
    sent = outer_blocks(order[half:], weighted, tokens, width)
    moved = swap(sent, "dp", flips[0])
    kept = outer_blocks(order[:half], weighted, tokens, width)
    total = kept.astype(F32) + moved.astype(F32)
    for flip in flips[1:]:
        half //= 2
        moved = swap(total[half:].astype(BF16), "dp", flip)
        total = total[:half] + moved.astype(F32)
    return total[0]


def local(inputs, cotangent, adapter_down, adapter_up, domain_ids, prior_weights):
    sections = lax.axis_size("segment")
    own = lax.axis_index("segment")
    owners = lax.axis_size("dp")
    owner = lax.axis_index("dp")
    rows, width = inputs.shape
    down, up = adapter_down[0], adapter_up[0]
    rank = down.shape[0]
    train = prior_weights.shape[0]
    domains = train + 1
    micros = domain_ids.shape[0] // owners
    tokens_of_micro = rows // micros
    chunk = width // owners
    order = jnp.asarray(reversed_bits(owners)) ^ owner

    up_block = lax.dynamic_slice_in_dim(up, owner * chunk, chunk, 0)
    down_block = lax.dynamic_slice_in_dim(down, owner * chunk, chunk, 1)
    up_from = [up_block] + [swap(up_block, "segment", e) for e in range(1, sections)]
    first = nt(inputs, down)
    last = nn(cotangent, up)
    pair = jnp.concatenate([first, last], axis=1).astype(BF16)
    pairs = [pair] + [swap(pair, "segment", e) for e in range(1, sections)]
    links = jnp.stack(
        [lax.dot_general(up_from[d], down_block, (((0,), (1,)), ((), ())), preferred_element_type=F32) for d in range(1, sections)]
    )
    links = all_sum(links, "dp").astype(BF16)
    links = [links] + [swap(links, "segment", e) for e in range(1, sections)]

    inner, acts = recurrence(own.reshape(1), pairs, links)
    inner32 = inner.astype(F32)
    earlier = [own ^ d for d in range(1, sections)]
    acts_from = [
        jnp.where(r < own, lax.dynamic_index_in_dim(acts, r, 0, keepdims=False), 0).astype(BF16) for r in earlier
    ]
    acts_wide = jnp.concatenate(acts_from, axis=1)
    ups_wide = jnp.concatenate(up_from[1:], axis=1)

    domain_range = jnp.arange(domains, dtype=jnp.int32)
    counts = jnp.sum((domain_ids[:, None] == domain_range[None, :]).astype(F32), axis=0)
    inverse = 1.0 / (counts * tokens_of_micro)
    local_ids = lax.dynamic_slice_in_dim(domain_ids, owner * micros, micros)
    token_ids = jnp.repeat(local_ids, tokens_of_micro)
    hot = (token_ids[:, None] == domain_range[None, :]).astype(F32)
    scale = jnp.sum(hot * inverse[None, :], axis=1)

    gen_weighted = (inner32 * (scale * hot[:, domains - 1])[:, None]).astype(BF16)
    gen_low = all_sum(tn(gen_weighted, acts_wide), "dp").astype(BF16)
    gen_own = scatter_sum(order, gen_weighted, inputs, chunk) + nt(gen_low, ups_wide)
    gen_square = jnp.sum(gen_own * gen_own)
    piece = gen_own.astype(BF16)[None]
    gen_up = all_sum(nn(piece[0], ups_wide), "dp").astype(BF16)
    aligned = project_blocks(order[:1], piece, inputs)
    for flip in reversed(bits_of(owners)):
        moved = swap(piece, "dp", flip)
        at = piece.shape[0]
        aligned = aligned + project_blocks(order[at : 2 * at], moved, inputs)
        piece = jnp.concatenate([piece, moved])
    aligned = aligned + nt(acts_wide, gen_up)
    per_token = jnp.sum(inner32 * aligned, axis=1) * scale
    scores = jnp.sum(hot[:, :train] * per_token[:, None], axis=0)
    figures = jnp.zeros((8, 128), F32).at[0, :train].set(scores).at[1, 0].set(gen_square)
    for axis in ("segment", "dp"):
        figures = all_sum(figures, axis, F32)
    scores, gen_square = figures[0, :train], figures[1, 0]

    entries = sections * rank * width
    mean_gen = gen_square / entries
    z = scores / (jnp.sqrt(F32(entries)) * (mean_gen + 1e-06))
    raised = prior_weights * jnp.exp(4.0 * jnp.tanh(z / 4.0))
    weights = SMOOTHING / train + (1.0 - SMOOTHING) * raised / jnp.sum(raised)

    token_weight = jnp.sum(hot[:, :train] * weights[None, :], axis=1) * scale
    weighted = (inner32 * token_weight[:, None]).astype(BF16)
    low = all_sum(tn(weighted, acts_wide), "dp").astype(BF16)
    mixed = scatter_sum(order, weighted, inputs, chunk) + nt(low, ups_wide)
    return weights, mixed[None]


def solution(mesh):
    return jax.shard_map(
        local,
        mesh=mesh,
        in_specs=(
            P("dp", None),
            P("dp", None),
            P("segment", None, None),
            P("segment", None, None),
            P(),
            P(),
        ),
        out_specs=(P(), P("segment", None, "dp")),
        check_vma=False,
    )
```

```python
import functools

import jax
import jax.numpy as jnp
import numpy as np
from jax import lax
from jax.experimental import pallas as pl
from jax.experimental.pallas import tpu as pltpu
from jax.sharding import PartitionSpec as P

SMOOTHING = 0.5
BF16 = jnp.bfloat16
F32 = jnp.float32


def swap(array, axis, flip):
    size = lax.axis_size(axis)
    return lax.ppermute(array, axis, [(i, i ^ flip) for i in range(size)])


def bits_of(size):
    return [1 << b for b in range(size.bit_length() - 1)]


def all_sum(array, axis, wire=BF16):
    for flip in bits_of(lax.axis_size(axis)):
        array = array + swap(array.astype(wire), axis, flip).astype(F32)
    return array


def reversed_bits(size):
    width = size.bit_length() - 1
    return np.array([int(format(p, f"0{width}b")[::-1], 2) if width else 0 for p in range(size)], np.int32)


def sigmoid(v):
    return 1.0 / (1.0 + jnp.exp(-v))


def nt(a, b):
    return lax.dot_general(a, b, (((1,), (1,)), ((), ())), preferred_element_type=F32)


def nn(a, b):
    return lax.dot_general(a, b, (((1,), (0,)), ((), ())), preferred_element_type=F32)


def tn(a, b):
    return lax.dot_general(a, b, (((0,), (0,)), ((), ())), preferred_element_type=F32)


def recurrence_kernel(sections, rank, slots, micro, own_ref, place, held, *refs):
    trios = refs[:sections]
    links = refs[sections : 2 * sections]
    scale, inner_out, act_out, pack_out = refs[2 * sections : 2 * sections + 4]
    trio_at, link_at, act_at, pre_at, inner_at = refs[2 * sections + 4 :]
    own = own_ref[0]
    for e in range(sections):
        trio_at[own ^ e] = trios[e][...]
        link_at[own ^ e] = links[e][...]
    for s in range(sections):
        pre = trio_at[s, :, :rank].astype(F32)
        for r in range(s):
            pre = pre + nn(act_at[r], link_at[s, (r ^ s) - 1])
        pre_at[s] = pre
        act_at[s] = (pre * sigmoid(pre)).astype(BF16)
    for s in reversed(range(sections)):
        pulled = trio_at[s, :, rank : 2 * rank].astype(F32)
        for r in range(s + 1, sections):
            pulled = pulled + nt(inner_at[r], link_at[r, (r ^ s) - 1])
        pre = pre_at[s]
        gate = sigmoid(pre)
        inner_at[s] = (pulled * (gate * (1.0 + pre * (1.0 - gate)))).astype(BF16)
    inner = inner_at[own].astype(F32)
    inner_out[...] = inner_at[own]
    pack_at = pre_at.at[0]
    pack_at[...] = inner * scale[...]
    gen = pack_at[...].astype(BF16)
    for k in range(slots):
        rows = pack_at[pl.ds(pl.multiple_of(place[k] * micro, 8), micro), :]
        pack_out[k * micro : (k + 1) * micro, :] = jnp.where(held[k] > 0, rows, 0.0).astype(BF16)
    at = slots * micro
    for d in range(1, sections):
        r = own ^ d
        act = jnp.where(r < own, act_at[r], jnp.zeros_like(act_at[r]))
        act_out[:, (d - 1) * rank : d * rank] = act
        pack_out[at : at + rank, :] = tn(gen, act).astype(BF16)
        pack_out[at + rank : at + 2 * rank, :] = tn(gen, trios[d][:, 2 * rank :]).astype(BF16)
        at += 2 * rank


def recurrence(own, place, held, trios, links, gen_scale, micro):
    sections, slots = len(trios), place.shape[0]
    rows, rank = trios[0].shape[0], trios[0].shape[1] // 3
    vmem = pl.BlockSpec(memory_space=pltpu.VMEM)
    smem = pl.BlockSpec(memory_space=pltpu.SMEM)
    return pl.pallas_call(
        functools.partial(recurrence_kernel, sections, rank, slots, micro),
        out_shape=(
            jax.ShapeDtypeStruct((rows, rank), BF16),
            jax.ShapeDtypeStruct((rows, (sections - 1) * rank), BF16),
            jax.ShapeDtypeStruct((slots * micro + 2 * (sections - 1) * rank, rank), BF16),
        ),
        in_specs=[smem] * 3 + [vmem] * (2 * sections + 1),
        out_specs=(vmem,) * 3,
        scratch_shapes=[
            pltpu.VMEM((sections, rows, 3 * rank), BF16),
            pltpu.VMEM((sections, sections - 1, rank, rank), BF16),
            pltpu.VMEM((sections, rows, rank), BF16),
            pltpu.VMEM((sections, rows, rank), F32),
            pltpu.VMEM((sections, rows, rank), BF16),
        ],
        name="recurrence",
    )(own, place, held, *trios, *links, gen_scale)


def pick_kernel(place, held, order, x_ref, o_ref):
    block = x_ref[...]
    o_ref[0] = jnp.where(held[pl.program_id(1)] > 0, block, jnp.zeros_like(block))


def pick_blocks(place, held, order, tokens, micro, width):
    count, slots = order.shape[0], place.shape[0]
    return pl.pallas_call(
        pick_kernel,
        out_shape=jax.ShapeDtypeStruct((count, slots * micro, width), BF16),
        grid_spec=pltpu.PrefetchScalarGridSpec(
            num_scalar_prefetch=3,
            grid=(count, slots),
            in_specs=[pl.BlockSpec((micro, width), lambda k, m, p, h, o: (p[m], o[k]))],
            out_specs=pl.BlockSpec((1, micro, width), lambda k, m, p, h, o: (k, m, 0)),
        ),
        cost_estimate=pl.CostEstimate(
            flops=0, bytes_accessed=4 * count * slots * micro * width, transcendentals=0
        ),
        name="pick_blocks",
    )(place, held, order, tokens)


def score_kernel(sections, rank, rows_gen, *refs):
    cross = refs[:sections]
    pack, cross_up, trail, act, inner, weight, o_ref = refs[sections:]
    base = sections * rows_gen
    aligned = nn(cross[0][...], pack[:rows_gen, :])
    for e in range(1, sections):
        aligned += nn(cross[e][...], pack[e * rows_gen : (e + 1) * rows_gen, :])
    for d in range(sections - 1):
        low = pack[base + 2 * d * rank + rank : base + 2 * d * rank + 2 * rank, :].astype(F32)
        for c in range(sections - 1):
            low += nn(
                pack[base + 2 * c * rank : base + 2 * c * rank + rank, :],
                cross_up[c * rank : (c + 1) * rank, d * rank : (d + 1) * rank],
            )
        aligned += nt(act[:, d * rank : (d + 1) * rank], low.astype(BF16))
        aligned += nt(trail[d][...], pack[base + 2 * d * rank : base + 2 * d * rank + rank, :])
    per_token = jnp.sum(inner[...].astype(F32) * aligned, axis=1, keepdims=True)
    o_ref[...] = jnp.broadcast_to(jnp.sum(per_token * weight[...], axis=0, keepdims=True), o_ref.shape)


def score_sums(cross, pack, cross_up, trios, act, inner, weight):
    sections, rank = len(cross), inner.shape[1]
    rows, rows_gen = cross[0].shape

    def kernel(*refs):
        trails = [ref.at[:, 2 * rank :] for ref in refs[sections + 2 : 2 * sections + 1]]
        score_kernel(sections, rank, rows_gen, *refs[: sections + 2], trails, *refs[2 * sections + 1 :])

    return pl.pallas_call(
        kernel,
        out_shape=jax.ShapeDtypeStruct((8, 128), F32),
        in_specs=[pl.BlockSpec(memory_space=pltpu.VMEM)] * (2 * sections + 4),
        out_specs=pl.BlockSpec(memory_space=pltpu.VMEM),
        name="score_sums",
    )(*cross, pack, cross_up, *trios[1:], act, inner, weight)


def outer_kernel(order, w_ref, x_ref, o_ref):
    o_ref[0] = tn(w_ref[...], x_ref[...]).astype(o_ref.dtype)


def outer_blocks(order, weighted, tokens, width):
    count, rows, rank = order.shape[0], weighted.shape[0], weighted.shape[1]
    return pl.pallas_call(
        outer_kernel,
        out_shape=jax.ShapeDtypeStruct((count, rank, width), BF16),
        grid_spec=pltpu.PrefetchScalarGridSpec(
            num_scalar_prefetch=1,
            grid=(count,),
            in_specs=[
                pl.BlockSpec((rows, rank), lambda k, o: (0, 0)),
                pl.BlockSpec((rows, width), lambda k, o: (0, o[k])),
            ],
            out_specs=pl.BlockSpec((1, rank, width), lambda k, o: (k, 0, 0)),
        ),
        cost_estimate=pl.CostEstimate(
            flops=2 * count * rows * rank * width,
            bytes_accessed=2 * count * width * (rows + rank),
            transcendentals=0,
        ),
        name="outer_blocks",
    )(order, weighted, tokens)


def project_kernel(order, g_ref, x_ref, o_ref):
    @pl.when(pl.program_id(0) == 0)
    def _():
        o_ref[...] = jnp.zeros_like(o_ref)

    o_ref[...] += nt(x_ref[...], g_ref[0])


def project_blocks(order, grads, tokens):
    count, rank, width = grads.shape
    rows = tokens.shape[0]
    return pl.pallas_call(
        project_kernel,
        out_shape=jax.ShapeDtypeStruct((rows, rank), F32),
        grid_spec=pltpu.PrefetchScalarGridSpec(
            num_scalar_prefetch=1,
            grid=(count,),
            in_specs=[
                pl.BlockSpec((1, rank, width), lambda k, o: (k, 0, 0)),
                pl.BlockSpec((rows, width), lambda k, o: (0, o[k])),
            ],
            out_specs=pl.BlockSpec((rows, rank), lambda k, o: (0, 0)),
        ),
        cost_estimate=pl.CostEstimate(
            flops=2 * count * rows * rank * width,
            bytes_accessed=2 * count * width * (rows + rank),
            transcendentals=0,
        ),
        name="project_blocks",
    )(order, grads, tokens)


def scatter_sum(order, weighted, tokens, width):
    size = order.shape[0]
    flips = bits_of(size)
    half = size // 2
    sent = outer_blocks(order[half:], weighted, tokens, width)
    moved = swap(sent, "dp", flips[0])
    kept = outer_blocks(order[:half], weighted, tokens, width)
    total = kept.astype(F32) + moved.astype(F32)
    for flip in flips[1:]:
        half //= 2
        moved = swap(total[half:].astype(BF16), "dp", flip)
        total = total[:half] + moved.astype(F32)
    return total[0]


def exchange_halves(array, bit, axis, flip):
    half = array.shape[0] // 2
    moved = swap(lax.dynamic_slice_in_dim(array, (1 - bit) * half, half), axis, flip)
    return lax.dynamic_slice_in_dim(array, bit * half, half), moved


def halved_sum(array, owner):
    flips = bits_of(lax.axis_size("dp"))
    bit = owner & 1
    kept, moved = exchange_halves(array, bit, "dp", flips[0])
    total = kept.astype(F32) + moved.astype(F32)
    for flip in flips[1:]:
        total = total + swap(total.astype(BF16), "dp", flip).astype(F32)
    total = total.astype(BF16)
    other = swap(total, "dp", flips[0])
    return jnp.concatenate([jnp.where(bit == 0, total, other), jnp.where(bit == 0, other, total)])


def spread_rows(place, held, order, tokens, micro, width):
    flips = bits_of(order.shape[0])
    half = order.shape[0] // 2
    moved = swap(pick_blocks(place, held, order[half:], tokens, micro, width), "dp", flips[0])
    piece = pick_blocks(place, held, order[:half], tokens, micro, width) + moved
    for flip in flips[1:]:
        half //= 2
        piece = piece[:half] + swap(piece[half:], "dp", flip)
    for flip in reversed(flips):
        piece = jnp.concatenate([piece, swap(piece, "dp", flip)])
    return piece


def local(inputs, cotangent, adapter_down, adapter_up, domain_ids, prior_weights):
    sections = lax.axis_size("segment")
    own = lax.axis_index("segment")
    owners = lax.axis_size("dp")
    owner = lax.axis_index("dp")
    rows, width = inputs.shape
    down, up = adapter_down[0], adapter_up[0]
    rank = down.shape[0]
    train = prior_weights.shape[0]
    domains = train + 1
    micros_all = domain_ids.shape[0]
    micros = micros_all // owners
    micro = rows // micros
    chunk = width // owners
    order = jnp.asarray(reversed_bits(owners)) ^ owner
    peers = range(1, sections)

    domain_range = jnp.arange(domains, dtype=jnp.int32)
    hot_all = domain_ids[:, None] == domain_range[None, :]
    counts = jnp.sum(hot_all.astype(F32), axis=0)
    inverse = 1.0 / (counts * micro)
    local_ids = lax.dynamic_slice_in_dim(domain_ids, owner * micros, micros)
    token_ids = jnp.repeat(local_ids, micro)
    hot = (token_ids[:, None] == domain_range[None, :]).astype(F32)
    scale = jnp.sum(hot * inverse[None, :], axis=1)
    share = -(-micros_all // (domains * sections))
    is_gen = hot_all[:, domains - 1].astype(jnp.int32)
    earlier = jnp.arange(micros_all)[None, :] < jnp.arange(micros_all)[:, None]
    nth = jnp.sum(jnp.where(earlier, is_gen[None, :], 0), axis=1)
    slot = jnp.concatenate([(own ^ e) * share + jnp.arange(share) for e in range(sections)])
    match = (nth[None, :] == slot[:, None]) & (is_gen[None, :] > 0)
    local_at = jnp.sum(jnp.where(match, jnp.arange(micros_all)[None, :], 0), axis=1) - owner * micros
    held = (jnp.any(match, axis=1) & (local_at >= 0) & (local_at < micros)).astype(jnp.int32)
    place = jnp.clip(local_at, 0, micros - 1).astype(jnp.int32)

    up_block = lax.dynamic_slice_in_dim(up, owner * chunk, chunk, 0)
    down_block = lax.dynamic_slice_in_dim(down, owner * chunk, chunk, 1)
    up_from = [swap(up_block, "segment", e) for e in peers]
    ups_wide = jnp.concatenate(up_from, axis=1)
    trio = jnp.concatenate([nt(inputs, down), nn(cotangent, up), nn(inputs, up)], axis=1).astype(BF16)
    trios = [trio] + [swap(trio, "segment", e) for e in peers]
    links = jnp.stack(
        [lax.dot_general(u, down_block, (((0,), (1,)), ((), ())), preferred_element_type=F32) for u in up_from]
    )
    links = all_sum(links, "dp").astype(BF16)
    links = [links] + [swap(links, "segment", e) for e in peers]
    cross_up = halved_sum(tn(ups_wide, ups_wide).astype(BF16), owner)

    gen_rows = spread_rows(place[:share], held[:share], order, inputs, micro, chunk)
    cross = project_blocks(order, gen_rows, inputs).astype(BF16)
    cross = [cross] + [swap(cross, "segment", e) for e in peers]

    gen_scale = (scale * hot[:, domains - 1])[:, None]
    inner, acts_wide, pack = recurrence(own.reshape(1), place, held, trios, links, gen_scale, micro)
    pack = halved_sum(pack, owner)
    weight = jnp.pad(hot * scale[:, None], ((0, 0), (0, 128 - domains)))
    figures = score_sums(cross, pack, cross_up, trios, acts_wide, inner, weight)
    for axis in ("segment", "dp"):
        figures = all_sum(figures, axis, F32)
    scores, gen_square = figures[0, :train], figures[0, train]

    entries = sections * rank * width
    mean_gen = gen_square / entries
    z = scores / (jnp.sqrt(F32(entries)) * (mean_gen + 1e-06))
    raised = prior_weights * jnp.exp(4.0 * jnp.tanh(z / 4.0))
    weights = SMOOTHING / train + (1.0 - SMOOTHING) * raised / jnp.sum(raised)

    token_weight = jnp.sum(hot[:, :train] * weights[None, :], axis=1) * scale
    weighted = (inner.astype(F32) * token_weight[:, None]).astype(BF16)
    low = all_sum(tn(weighted, acts_wide), "dp").astype(BF16)
    mixed = scatter_sum(order, weighted, inputs, chunk) + nt(low, ups_wide)
    return weights, mixed[None]


def solution(mesh):
    return jax.shard_map(
        local,
        mesh=mesh,
        in_specs=(
            P("dp", None),
            P("dp", None),
            P("segment", None, None),
            P("segment", None, None),
            P(),
            P(),
        ),
        out_specs=(P(), P("segment", None, "dp")),
        check_vma=False,
    )
```

```python
import functools

import jax
import jax.numpy as jnp
from jax import lax
from jax.experimental import pallas as pl
from jax.experimental.pallas import tpu as pltpu
from jax.sharding import PartitionSpec as P

SMOOTHING = 0.5
BF16 = jnp.bfloat16
F32 = jnp.float32
I32 = jnp.int32
VMEM = pl.BlockSpec(memory_space=pltpu.VMEM)
SMEM = pl.BlockSpec(memory_space=pltpu.SMEM)


def call(kernel, outs, ins, name, work=1, scratch=(), limit=20):
    arrays, specs = [], []
    for item in ins:
        array, spec = item if isinstance(item, tuple) else (item, VMEM)
        arrays.append(array)
        specs.append(spec)
    shapes, out_specs = [], []
    for item in outs:
        shape, dtype, spec = item if len(item) == 3 else (*item, VMEM)
        shapes.append(jax.ShapeDtypeStruct(shape, dtype))
        out_specs.append(spec)
    return pl.pallas_call(
        kernel,
        out_shape=tuple(shapes),
        in_specs=specs,
        out_specs=tuple(out_specs),
        scratch_shapes=list(scratch),
        cost_estimate=pl.CostEstimate(
            flops=int(work * 400e6), bytes_accessed=int(work * 2e6), transcendentals=0
        ),
        compiler_params=pltpu.CompilerParams(vmem_limit_bytes=limit << 20),
        name=name,
    )(*arrays)


def swap(array, axis, flip):
    size = lax.axis_size(axis)
    return lax.ppermute(array, axis, [(i, i ^ flip) for i in range(size)])


def bits_of(size):
    return [1 << b for b in range(size.bit_length() - 1)]


def reversed_bits(size):
    width = size.bit_length() - 1
    return [int(format(p, f"0{width}b")[::-1], 2) if width else 0 for p in range(size)]


def all_sum(array, axis, wire=BF16):
    for flip in bits_of(lax.axis_size(axis)):
        array = array + swap(array.astype(wire), axis, flip).astype(F32)
    return array


def halved_sum(array):
    flips = bits_of(lax.axis_size("dp"))
    bit = lax.axis_index("dp") & 1
    half = array.shape[0] // 2
    moved = swap(lax.dynamic_slice_in_dim(array, (1 - bit) * half, half), "dp", flips[0])
    total = lax.dynamic_slice_in_dim(array, bit * half, half).astype(F32) + moved.astype(F32)
    for flip in flips[1:]:
        total = total + swap(total.astype(BF16), "dp", flip).astype(F32)
    total = total.astype(BF16)
    other = swap(total, "dp", flips[0])
    return jnp.concatenate([jnp.where(bit == 0, total, other), jnp.where(bit == 0, other, total)])


def sigmoid(v):
    return 1.0 / (1.0 + jnp.exp(-v))


def nt(a, b):
    return lax.dot_general(a, b, (((1,), (1,)), ((), ())), preferred_element_type=F32)


def nn(a, b):
    return lax.dot_general(a, b, (((1,), (0,)), ((), ())), preferred_element_type=F32)


def tn(a, b):
    return lax.dot_general(a, b, (((0,), (0,)), ((), ())), preferred_element_type=F32)


def block_of(rel, chunk):
    return pl.ds(pl.multiple_of((lax.axis_index("dp") ^ rel) * chunk, chunk), chunk)


def make_plan(ids, domains, slots, share, micros, micro):
    total = ids.shape[0]

    def kernel(ids_ref, plan, scale, count, where):
        own, owner = lax.axis_index("segment"), lax.axis_index("dp")
        for i in range(domains):
            count[i] = 0
        for k in range(total):
            where[k] = 0

        def step(m, carry):
            d = ids_ref[m]
            c = count[d]

            @pl.when(d == domains - 1)
            def _():
                where[c] = m

            count[d] = c + 1
            return carry

        lax.fori_loop(0, total, step, 0)
        present = count[domains - 1]
        for k in range(slots):
            slot = (own ^ (k // share)) * share + k % share
            at = where[jnp.minimum(slot, total - 1)] - owner * micros
            plan[slots + k] = ((slot < present) & (at >= 0) & (at < micros)).astype(I32)
            plan[k] = jnp.clip(at, 0, micros - 1)
        for m in range(micros):
            d = ids_ref[owner * micros + m]
            plan[2 * slots + m] = d
            scale[m] = 1.0 / (count[d].astype(F32) * micro)

    return call(
        kernel,
        [((2 * slots + micros,), I32, SMEM), ((micros,), F32, SMEM)],
        [(ids, SMEM)],
        "make_plan",
        scratch=[pltpu.SMEM((domains,), I32), pltpu.SMEM((total,), I32)],
    )


def pick_rows(plan, x, share, slots, micro, chunk, rels):
    size = len(rels)
    half = size // 2

    def kernel(plan_ref, x_ref, sent, kept):
        for m in range(share):
            rows = pl.ds(pl.multiple_of(plan_ref[m] * micro, 8), micro)
            on = plan_ref[slots + m] > 0
            for p, rel in enumerate(rels):
                block = x_ref[rows, block_of(rel, chunk)]
                block = jnp.where(on, block, jnp.zeros_like(block))
                out = kept.at[p] if p < half else sent.at[p - half]
                out[m * micro : (m + 1) * micro, :] = block

    shape = (half, share * micro, chunk)
    return call(kernel, [(shape, BF16), (shape, BF16)], [(plan, SMEM), x], "pick_rows", 2)


def token_products(x, cotangent, down, up):
    rows, rank = x.shape[0], down.shape[0]

    def kernel(x_ref, c_ref, d_ref, u_ref, out):
        out[:, :rank] = nt(x_ref[...], d_ref[...]).astype(BF16)
        out[:, rank : 2 * rank] = nn(c_ref[...], u_ref[...]).astype(BF16)
        out[:, 2 * rank :] = nn(x_ref[...], u_ref[...]).astype(BF16)

    return call(kernel, [((rows, 3 * rank), BF16)], [x, cotangent, down, up], "token_products", 7)[0]


def weight_products(ups, down, chunk):
    rank, peers = down.shape[0], len(ups)

    def kernel(*refs):
        u, d_ref, links, cross = refs[:peers], refs[peers], refs[peers + 1], refs[peers + 2]
        block = d_ref[:, block_of(0, chunk)]
        for i in range(peers):
            left = u[i][...].T
            links[i] = nt(left, block)
            for j in range(peers):
                cross[i * rank : (i + 1) * rank, j * rank : (j + 1) * rank] = nn(left, u[j][...]).astype(BF16)

    return call(
        kernel,
        [((peers, rank, rank), F32), ((peers * rank, peers * rank), BF16)],
        [*ups, down],
        "weight_products",
        2,
    )


def recurrence(plan, scale, trios, links, domains, slots, micro):
    sections = len(trios)
    rows, rank = trios[0].shape[0], trios[0].shape[1] // 3
    micros = rows // micro

    def kernel(plan_ref, scale_ref, *refs):
        trio, link = refs[:sections], refs[sections : 2 * sections]
        inner_out, act_out, pack_out = refs[2 * sections : 2 * sections + 3]
        trio_at, link_at, act_at, pre_at, inner_at = refs[2 * sections + 3 :]
        own = lax.axis_index("segment")
        for e in range(sections):
            trio_at[own ^ e] = trio[e][...]
            link_at[own ^ e] = link[e][...]
        for s in range(sections):
            pre = trio_at[s, :, :rank].astype(F32)
            for r in range(s):
                pre = pre + nn(act_at[r], link_at[s, (r ^ s) - 1])
            pre_at[s] = pre
            act_at[s] = (pre * sigmoid(pre)).astype(BF16)
        for s in reversed(range(sections)):
            pulled = trio_at[s, :, rank : 2 * rank].astype(F32)
            for r in range(s + 1, sections):
                pulled = pulled + nt(inner_at[r], link_at[r, (r ^ s) - 1])
            pre = pre_at[s]
            gate = sigmoid(pre)
            inner_at[s] = (pulled * (gate * (1.0 + pre * (1.0 - gate)))).astype(BF16)
        inner = inner_at[own]
        inner_out[...] = inner
        wide = pre_at.at[0]
        gen = pre_at.at[1]
        last = domains - 1
        for m in range(micros):
            span = slice(m * micro, (m + 1) * micro)
            scaled = inner_at[own, span, :].astype(F32) * scale_ref[m]
            wide[span, :] = scaled
            gen[span, :] = jnp.where(plan_ref[2 * slots + m] == last, scaled, 0.0)
        for k in range(slots):
            picked = wide[pl.ds(pl.multiple_of(plan_ref[k] * micro, 8), micro), :]
            on = plan_ref[slots + k] > 0
            pack_out[k * micro : (k + 1) * micro, :] = jnp.where(on, picked, 0.0).astype(BF16)
        left = gen[...].astype(BF16).T
        at = slots * micro
        for d in range(1, sections):
            r = own ^ d
            act = jnp.where(r < own, act_at[r], jnp.zeros((rows, rank), BF16))
            act_out[:, (d - 1) * rank : d * rank] = act
            pack_out[at : at + rank, :] = nn(left, act).astype(BF16)
            pack_out[at + rank : at + 2 * rank, :] = nn(left, trio[d][:, 2 * rank :]).astype(BF16)
            at += 2 * rank

    return call(
        kernel,
        [
            ((rows, rank), BF16),
            ((rows, (sections - 1) * rank), BF16),
            ((slots * micro + 2 * (sections - 1) * rank, rank), BF16),
        ],
        [(plan, SMEM), (scale, SMEM), *trios, *links],
        "recurrence",
        4,
        scratch=[
            pltpu.VMEM((sections, rows, 3 * rank), BF16),
            pltpu.VMEM((sections, sections - 1, rank, rank), BF16),
            pltpu.VMEM((sections, rows, rank), BF16),
            pltpu.VMEM((sections, rows, rank), F32),
            pltpu.VMEM((sections, rows, rank), BF16),
        ],
    )


def project(x, pieces, rels, chunk, before=None):
    rows, wide = x.shape[0], pieces[0].shape[1]
    dtype = F32 if before is None else BF16

    def kernel(x_ref, *refs):
        out = refs[-1]
        total = jnp.zeros((rows, wide), F32) if before is None else refs[0][...]
        at = 0
        for piece in refs[before is not None : -1]:
            for i in range(piece.shape[0]):
                total = total + nt(x_ref[:, block_of(rels[at], chunk)], piece[i])
                at += 1
        out[...] = total.astype(dtype)

    head = [] if before is None else [before]
    return call(kernel, [((rows, wide), dtype)], [x, *head, *pieces], "project", 2)[0]


def spread_rows(x, plan, share, slots, micro, chunk, rels):
    flips = bits_of(len(rels))
    half = len(rels) // 2
    sent, piece = pick_rows(plan, x, share, slots, micro, chunk, rels)
    piece = piece + swap(sent, "dp", flips[0])
    for flip in flips[1:]:
        half //= 2
        piece = piece[:half] + swap(piece[half:], "dp", flip)
    pieces = [piece]
    for flip in reversed(flips[1:]):
        pieces.append(swap(jnp.concatenate(pieces), "dp", flip))
    far = swap(jnp.concatenate(pieces), "dp", flips[0])
    half = len(rels) // 2
    before = project(x, pieces, rels[:half], chunk)
    return project(x, [far], rels[half:], chunk, before)


def score_sums(plan, scale, cross, pack, cross_up, trios, acts, inner, slots, micro):
    sections, rank = len(cross), inner.shape[1]
    rows, wide = cross[0].shape
    micros = rows // micro
    base = sections * wide

    def kernel(plan_ref, scale_ref, *refs):
        cr, (pk, cu), trail = refs[:sections], refs[sections : sections + 2], refs[sections + 2 : 2 * sections + 1]
        act, inn, out = refs[2 * sections + 1 :]
        aligned = nn(cr[0][...], pk[:wide, :])
        for e in range(1, sections):
            aligned += nn(cr[e][...], pk[e * wide : (e + 1) * wide, :])
        for d in range(sections - 1):
            at = base + 2 * d * rank
            low = pk[at + rank : at + 2 * rank, :].astype(F32)
            for c in range(sections - 1):
                first = base + 2 * c * rank
                low += nn(pk[first : first + rank, :], cu[c * rank : (c + 1) * rank, d * rank : (d + 1) * rank])
            aligned += nt(act[:, d * rank : (d + 1) * rank], low.astype(BF16))
            aligned += nt(trail[d][:, 2 * rank :], pk[at : at + rank, :])
        product = inn[...].astype(F32) * aligned
        lane = lax.broadcasted_iota(I32, (1, 128), 1)
        total = jnp.zeros((1, 128), F32)
        for m in range(micros):
            part = jnp.sum(product[m * micro : (m + 1) * micro], axis=0, keepdims=True)
            part = jnp.sum(part, axis=1, keepdims=True) * scale_ref[m]
            total = total + jnp.where(lane == plan_ref[2 * slots + m], part, 0.0)
        out[...] = jnp.broadcast_to(total, out.shape)

    return call(
        kernel,
        [((8, 128), F32)],
        [(plan, SMEM), (scale, SMEM), *cross, pack, cross_up, *trios[1:], acts, inner],
        "score_sums",
        3,
    )[0]


def reweigh(plan, scale, figures, moved, prior, inner, acts, x, slots, micro, chunk, rels, entries, train):
    rows, rank = inner.shape
    micros = rows // micro

    def kernel(plan_ref, scale_ref, f_ref, g_ref, p_ref, inn, act, x_ref, w_out, low, left_out, out):
        figure = f_ref[...] + g_ref[...]
        lane = lax.broadcasted_iota(I32, figure.shape, 1)
        square = jnp.sum(jnp.where(lane == train, figure, 0.0), axis=1, keepdims=True)
        z = figure / (jnp.sqrt(F32(entries)) * (square / entries + 1e-06))
        raised = jnp.where(lane < train, p_ref[...] * jnp.exp(4.0 * jnp.tanh(z / 4.0)), 0.0)
        share = raised / jnp.sum(raised, axis=1, keepdims=True)
        weights = jnp.where(lane < train, SMOOTHING / train + (1.0 - SMOOTHING) * share, 0.0)
        w_out[...] = weights
        parts = []
        for m in range(micros):
            mine = jnp.where(lane[:1] == plan_ref[2 * slots + m], weights[:1], 0.0)
            mine = jnp.sum(mine, axis=1, keepdims=True) * scale_ref[m]
            parts.append(inn[m * micro : (m + 1) * micro, :].astype(F32) * mine)
        left = jnp.concatenate(parts, axis=0).astype(BF16).T
        left_out[...] = left
        for p, rel in enumerate(rels):
            out[p] = nn(left, x_ref[:, block_of(rel, chunk)]).astype(BF16)
        low[...] = nn(left, act[...])

    return call(
        kernel,
        [
            ((8, 128), F32),
            ((rank, acts.shape[1]), F32),
            ((rank, rows), BF16),
            ((len(rels), rank, chunk), BF16),
        ],
        [(plan, SMEM), (scale, SMEM), figures, moved, prior, inner, acts, x],
        "reweigh",
        3,
    )


def outer_blocks(left, x, chunk, rels):
    rank = left.shape[0]

    def kernel(l_ref, x_ref, out):
        for p, rel in enumerate(rels):
            out[p] = nn(l_ref[...], x_ref[:, block_of(rel, chunk)]).astype(BF16)

    return call(kernel, [((len(rels), rank, chunk), BF16)], [left, x], "outer_blocks", 1.5)[0]


def finish(total, moved, low, far, ups):
    rank, chunk = total.shape

    def kernel(t_ref, m_ref, l_ref, f_ref, *refs):
        ups_ref, out = refs[:-1], refs[-1]
        value = t_ref[...] + m_ref[...].astype(F32)
        sums = (l_ref[...] + f_ref[...].astype(F32)).astype(BF16)
        for d, u in enumerate(ups_ref):
            value += nt(sums[:, d * rank : (d + 1) * rank], u[...])
        out[...] = value

    return call(kernel, [((rank, chunk), F32)], [total, moved, low, far, *ups], "finish", 1)[0]


def local(inputs, cotangent, adapter_down, adapter_up, domain_ids, prior_weights):
    sections = lax.axis_size("segment")
    owners = lax.axis_size("dp")
    owner = lax.axis_index("dp")
    rows, width = inputs.shape
    down, up = adapter_down[0], adapter_up[0]
    rank = down.shape[0]
    train = prior_weights.shape[0]
    domains = train + 1
    micros = domain_ids.shape[0] // owners
    micro = rows // micros
    chunk = width // owners
    share = -(-domain_ids.shape[0] // (domains * sections))
    slots = share * sections
    rels = reversed_bits(owners)
    flips = bits_of(owners)
    peers = range(1, sections)

    up_block = lax.dynamic_slice_in_dim(up, owner * chunk, chunk, 0)
    ups = [swap(up_block, "segment", e) for e in peers]
    plan, scale = make_plan(domain_ids, domains, slots, share, micros, micro)
    cross = spread_rows(inputs, plan, share, slots, micro, chunk, rels)
    trio = token_products(inputs, cotangent, down, up)
    trios = [trio] + [swap(trio, "segment", e) for e in peers]
    links, cross_up = weight_products(ups, down, chunk)
    links = all_sum(links, "dp").astype(BF16)
    links = [links] + [swap(links, "segment", e) for e in peers]
    cross_up = halved_sum(cross_up)
    cross = [cross] + [swap(cross, "segment", e) for e in peers]

    inner, acts, pack = recurrence(plan, scale, trios, links, domains, slots, micro)
    pack = halved_sum(pack)
    figures = score_sums(plan, scale, cross, pack, cross_up, trios, acts, inner, slots, micro)
    figures = all_sum(figures, "segment", F32)
    for flip in flips[:-1]:
        figures = figures + swap(figures, "dp", flip)
    moved = swap(figures, "dp", flips[-1])

    prior = jnp.broadcast_to(jnp.pad(prior_weights, (0, 128 - train))[None, :], (8, 128))
    half = owners // 2
    weights, low, left, sent = reweigh(
        plan, scale, figures, moved, prior, inner, acts, inputs, slots, micro, chunk, rels[half:], sections * rank * width, train
    )
    moved = swap(sent, "dp", flips[0])
    total = outer_blocks(left, inputs, chunk, rels[:half]).astype(F32) + moved.astype(F32)
    for flip in flips[1:-1]:
        half //= 2
        moved = swap(total[half:].astype(BF16), "dp", flip)
        total = total[:half] + moved.astype(F32)

    for flip in flips[:-1]:
        low = low + swap(low.astype(BF16), "dp", flip).astype(F32)
    far_low = swap(low.astype(BF16), "dp", flips[-1])
    moved = swap(total[1].astype(BF16), "dp", flips[-1])
    mixed = finish(total[0], moved, low, far_low, ups)
    return weights[0, :train], mixed[None]


def solution(mesh):
    return jax.shard_map(
        local,
        mesh=mesh,
        in_specs=(
            P("dp", None),
            P("dp", None),
            P("segment", None, None),
            P("segment", None, None),
            P(),
            P(),
        ),
        out_specs=(P(), P("segment", None, "dp")),
        check_vma=False,
    )
```
